32 devices in a mesh: chain: 2 (over x), slab: 16 (over z, y, core).
Axes of the slice: x: 2, y: 2, z: 4, core: 2. Of those that a mesh axis runs over, the one named last changes fastest.
Arguments:
- whitened: float32 [1024, 256, 256], P(('chain', 'slab')), parts along dimension 0, may hold values from -6 to 6
- counts: int32 [1024, 256, 256], P(('chain', 'slab')), parts along dimension 0, may hold values from 0 to 24
- exposure: int32 [1024, 256, 256], P(('chain', 'slab')), parts along dimension 0, may hold values from 1 to 12
- cholesky_east: float32 [512, 512], replicated, as said below
- cholesky_north: float32 [256, 256], replicated, as said below
- cholesky_time: float32 [256, 256], replicated, as said below
Outputs:
- gradient: float32 [1024, 256, 256], P(('chain', 'slab')), parts along dimension 0
- density: float32 [2], P('chain'), parts along dimension 0
The draws below stay inside these ranges and needn't reach their ends.
There are 2 independent parts, one for each index of `chain`. The reference program is written for one: setup_inputs(seed, part) draws one part's arguments, and reference() takes and returns one part's arrays. A program takes and returns all parts, laid end to end along the dimension named above; an argument that names none is the same for every part. Nothing has to cross between parts.
Inputs may be any that keep to these rules, and one draw needn't show every extreme that they name: `cholesky_east`: lower triangular with a positive diagonal, each row of unit length. `cholesky_north`: lower triangular with a positive diagonal, each row of unit length. `cholesky_time`: lower triangular with a positive diagonal, each row of unit length.
All inputs are finite; a program needn't handle non-finite values.
Results may differ from the reference program's by a relative error of at most 0.00008.
Values sent between devices are 32-bit elements; how exact they have to be, the bound alone decides.
A program may use at most 128 MiB of HBM per device.

```python
import jax
import jax.numpy as jnp
from jax import lax

NX = 512
NY = 256
NT = 256


def lower_factor(key, extent):
    key_off, key_diag = jax.random.split(key)
    random_part = jax.random.normal(key_off, (extent, extent), jnp.float32)
    row_index = lax.broadcasted_iota(jnp.int32, (extent, extent), 0)
    col_index = lax.broadcasted_iota(jnp.int32, (extent, extent), 1)
    spread = 0.6
    lower_part = jnp.where(col_index < row_index, random_part * spread / jnp.sqrt(row_index.astype(jnp.float32) + 1.0), 0.0)
    diagonal = jax.random.uniform(key_diag, (extent,), jnp.float32, 0.7, 1.3)
    lower_part = lower_part + jnp.diag(diagonal)
    return lower_part / jnp.sqrt(jnp.sum(lower_part * lower_part, axis=1, keepdims=True))


def draw_cholesky_east(key, part):
    return lower_factor(jax.random.fold_in(key, 101), NX)


def draw_cholesky_north(key, part):
    return lower_factor(jax.random.fold_in(key, 202), NY)


def draw_cholesky_time(key, part):
    return lower_factor(jax.random.fold_in(key, 303), NT)


def observed_pair(key):
    base_key = jax.random.fold_in(key, 404)
    key_exposure, key_counts = jax.random.split(base_key)
    east_index = lax.broadcasted_iota(jnp.int32, (NX, NY, NT), 0)
    exposure = jax.random.randint(key_exposure, (NX, NY, NT), 1, 5, dtype=jnp.int32) + 8 * east_index // NX
    counts = jax.random.randint(key_counts, (NX, NY, NT), 0, 2 * exposure + 1, dtype=jnp.int32)
    return (counts, exposure)


def draw_counts(key, part):
    return observed_pair(key)[0]


def draw_exposure(key, part):
    return observed_pair(key)[1]


def block_scale(rng, shape, cuts, low, top_value):
    level, own = 1.0, jax.random.fold_in(rng, 6)
    for axis_at, shards_of in cuts:
        draws = jnp.exp(jax.random.uniform(jax.random.fold_in(own, axis_at), (shards_of,), jnp.float32, low / len(cuts), top_value / len(cuts)))
        level = level * jnp.repeat(draws, shape[axis_at] // shards_of).reshape([-1 if axis == axis_at else 1 for axis in range(len(shape))])
    return level


def bell_draw(stream_key, dims, scale, limit, pieces=(), held_as=jnp.bfloat16):
    loudness = block_scale(stream_key, dims, pieces, -0.22, 0.18) if pieces else 1.0
    entries = jax.random.normal(stream_key, dims, jnp.float32) * scale * loudness
    return jnp.minimum(jnp.maximum(entries, -limit), limit).astype(held_as)


def setup_inputs(seed: int = 0, part: int = 0) -> dict:
    key_of = jax.random.split(jax.random.key(seed), 7)
    own_keys = jax.random.split(jax.random.fold_in(key_of[6], part), 7)
    whitened = bell_draw(own_keys[0], (NX, NY, NT), 1.0, 6.0, ((0, 16),), jnp.float32)
    counts = draw_counts(jax.random.fold_in(jax.random.fold_in(key_of[6], part), 71), part)
    exposure = draw_exposure(jax.random.fold_in(jax.random.fold_in(key_of[6], part), 71), part)
    cholesky_east = draw_cholesky_east(jax.random.fold_in(key_of[6], 71), part)
    cholesky_north = draw_cholesky_north(jax.random.fold_in(key_of[6], 71), part)
    cholesky_time = draw_cholesky_time(jax.random.fold_in(key_of[6], 71), part)
    return dict(whitened=whitened, counts=counts, exposure=exposure, cholesky_east=cholesky_east, cholesky_north=cholesky_north, cholesky_time=cholesky_time)


field_scale = 0.6


def mode_last(values, matrix):
    return jnp.einsum("abc,tc->abt", values, matrix, precision=lax.Precision.HIGHEST)


def mode_middle(values, matrix):
    return jnp.einsum("abc,yb->ayc", values, matrix, precision=lax.Precision.HIGHEST)


def mode_first(values, matrix):
    return jnp.einsum("abc,xa->xbc", values, matrix, precision=lax.Precision.HIGHEST)


def adjoint_last(values, matrix):
    return jnp.einsum("abt,tc->abc", values, matrix, precision=lax.Precision.HIGHEST)


def adjoint_middle(values, matrix):
    return jnp.einsum("ayc,yb->abc", values, matrix, precision=lax.Precision.HIGHEST)


def adjoint_first(values, matrix):
    return jnp.einsum("xbc,xa->abc", values, matrix, precision=lax.Precision.HIGHEST)


def reference(whitened, counts, exposure, cholesky_east, cholesky_north, cholesky_time):
    values = mode_first(mode_middle(mode_last(whitened, cholesky_time), cholesky_north), cholesky_east)
    log_rate = field_scale * values
    observed = counts.astype(jnp.float32)
    intensity = exposure.astype(jnp.float32) * jnp.exp(log_rate)
    residual = observed - intensity
    total_sum = jnp.sum(observed * log_rate - intensity) - 0.5 * jnp.sum(whitened * whitened)
    density = total_sum / (NX * NY * NT)
    adjoint = adjoint_last(adjoint_middle(adjoint_first(residual, cholesky_east), cholesky_north), cholesky_time)
    gradient = field_scale * adjoint - whitened
    return gradient, jnp.reshape(density, (1,))
```

```python
import functools

import jax
import jax.numpy as jnp
from jax import lax
from jax.experimental import pallas as pl
from jax.experimental.pallas import tpu as pltpu
from jax.sharding import PartitionSpec as P

field_scale = 0.6
QUARTERS = 4
LANES = 128
AHEAD = 12
DEPTH = 16
FORWARD_LAG = (1, 1, 2, 3)
BACKWARD_LAG = (7, 6, 5, 4)
VMEM_BYTES = 67043328


def split(values):
    high = values.astype(jnp.bfloat16)
    low = (values - high.astype(jnp.float32)).astype(jnp.bfloat16)
    return high, low


def hhl(matrix, axis):
    high, low = split(matrix)
    return jnp.concatenate([high, high, low], axis=axis)


def hlh(matrix, axis):
    high, low = split(matrix)
    return jnp.concatenate([high, low, high], axis=axis)


def dot(left, right):
    return jnp.dot(left, right, preferred_element_type=jnp.float32)


def kernel(
    group, parts, q_hbm, cnt_hbm, exp_hbm, east, prior, out_hbm, density,
    own, f0, f1, cnt, wgt, b0, b1, res, spare, out, fwd, bwd, acc, near, far,
    send_in, recv_p, recv_c, recv_e, send_z, recv_f0, recv_f1, recv_b0, recv_b1,
    send_r, send_s, send_g, keep_g, recv_g,
    send_near, recv_near, send_far, recv_far,
):
    slab = lax.axis_index("slab")
    quarter = slab // group
    place = slab % group
    chunks = own.shape[0]
    rows = own.shape[1]
    planes = q_hbm.shape[0]
    lines = q_hbm.shape[1] // group
    depth = res.shape[0]
    lanes = own.shape[2]

    def device(quarter_of, place_of):
        return {"slab": quarter_of * group + place_of}

    barrier = pltpu.get_barrier_semaphore()
    for j in range(1, group):
        pl.semaphore_signal(barrier, inc=1, device_id=device(quarter, lax.rem(place + j, group)), device_id_type=pl.DeviceIdType.MESH)
    for j in range(1, QUARTERS):
        pl.semaphore_signal(barrier, inc=1, device_id=device(lax.rem(quarter + j, QUARTERS), place), device_id_type=pl.DeviceIdType.MESH)
    pl.semaphore_wait(barrier, group + QUARTERS - 2)

    def remote(src, dst, send_sem, recv_sem, target):
        pltpu.make_async_remote_copy(
            src_ref=src, dst_ref=dst, send_sem=send_sem, recv_sem=recv_sem,
            device_id=target, device_id_type=pl.DeviceIdType.MESH,
        ).start()

    def await_bytes(ref, sem):
        pltpu.make_async_copy(ref, ref, sem).wait()

    def times_of(chunk):
        return pl.ds(pl.multiple_of(lax.rem(chunk, parts) * lanes, lanes), lanes)

    def spread(chunk):
        mine = pl.ds(place * planes, planes)
        line = chunk // parts
        for k, (src, dst, recv) in enumerate(((q_hbm, own, recv_p), (cnt_hbm, cnt, recv_c), (exp_hbm, wgt, recv_e))):
            for j in range(1, group):
                to = lax.rem(place + j, group)
                remote(
                    src.at[:, to * lines + line, times_of(chunk)], dst.at[chunk, mine],
                    send_in.at[k], recv.at[chunk], device(quarter, to),
                )
            pltpu.make_async_copy(
                src.at[:, place * lines + line, times_of(chunk)], dst.at[chunk, mine], recv.at[chunk]
            ).start()

    def collect(chunk, slot):
        there = (slice(None), place * lines + chunk // parts, times_of(chunk))
        for j in range(1, group):
            to = lax.rem(place + j, group)
            remote(out.at[slot, pl.ds(to * planes, planes)], out_hbm.at[there], send_g.at[slot], recv_g, device(quarter, to))
        pltpu.make_async_copy(out.at[slot, pl.ds(place * planes, planes)], out_hbm.at[there], keep_g.at[slot]).start()

    def await_collected(slot):
        if group > 1:
            await_bytes(out.at[slot, pl.ds(0, (group - 1) * planes)], send_g.at[slot])
        await_bytes(out.at[slot, pl.ds(0, planes)], keep_g.at[slot])

    def onward(q, chunk):
        await_bytes(own.at[chunk], recv_p.at[chunk])
        if q == 0:
            remote(own.at[chunk], f1.at[chunk], send_z.at[1], recv_f1.at[chunk], device(2, place))
            remote(own.at[chunk], f0.at[chunk], send_z.at[0], recv_f0.at[chunk], device(1, place))
        if q == 1:
            remote(own.at[chunk], f0.at[chunk], send_z.at[0], recv_f0.at[chunk], device(2, place))

    def forward(q, chunk):
        slot = lax.rem(chunk, depth)
        await_bytes(cnt.at[chunk], recv_c.at[chunk])
        await_bytes(wgt.at[chunk], recv_e.at[chunk])
        if q >= 1:
            await_bytes(f0.at[chunk], recv_f0.at[chunk])
        if q == 2:
            await_bytes(f1.at[chunk], recv_f1.at[chunk])

        @pl.when(chunk >= depth)
        def _():
            for _ in range((0, 0, 1, 2)[q]):
                await_bytes(res.at[slot], send_r.at[slot])
            if q == 2:
                await_bytes(spare.at[slot], send_s.at[slot])

        terms = ((own,), (f0, own), (f1, f0, own), (own,))[q]
        high_low = hlh(jnp.concatenate([ref[chunk] for ref in terms], axis=0), 0)
        count = 2 if q == 2 else 1
        field = dot(fwd[0 : count * rows, 0 : 3 * len(terms) * rows], high_low)
        if q == 2:
            spare[slot] = field[rows:]
            field = field[:rows]
        if q == 3:
            field = field + f0[chunk]
        log_rate = field_scale * field
        observed = cnt[chunk].astype(jnp.float32)
        intensity = wgt[chunk].astype(jnp.float32) * jnp.exp(log_rate)
        acc[...] += observed * log_rate - intensity
        res[slot] = observed - intensity
        if q == 2:
            remote(spare.at[slot], f0.at[chunk], send_s.at[slot], recv_f0.at[chunk], device(3, place))
            remote(res.at[slot], b0.at[chunk], send_r.at[slot], recv_b0.at[chunk], device(1, place))
        if q == 3:
            remote(res.at[slot], b1.at[chunk], send_r.at[slot], recv_b1.at[chunk], device(1, place))
            remote(res.at[slot], b0.at[chunk], send_r.at[slot], recv_b0.at[chunk], device(2, place))

    def backward(q, chunk):
        slot = lax.rem(chunk, depth)
        if q <= 2:
            await_bytes(b0.at[chunk], recv_b0.at[chunk])
        if q == 1:
            await_bytes(b1.at[chunk], recv_b1.at[chunk])

        @pl.when(chunk >= depth)
        def _():
            await_collected(slot)
            if q == 1:
                await_bytes(spare.at[slot], send_s.at[slot])

        terms = [res[slot]]
        if q in (1, 2):
            terms.append(b0[chunk])
        if q == 1:
            terms.append(b1[chunk])
        high_low = hlh(jnp.concatenate(terms, axis=0), 0)
        count = 2 if q == 1 else 1
        value = dot(bwd[0 : count * rows, 0 : 3 * len(terms) * rows], high_low)
        if q == 1:
            spare[slot] = value[rows:]
            remote(spare.at[slot], b0.at[chunk], send_s.at[slot], recv_b0.at[chunk], device(0, place))
            value = value[:rows]
        if q == 0:
            value = value + b0[chunk]
        out[slot] = value
        collect(chunk, slot)

    def block(r0, r1, c0, c1):
        return east[r0 * rows : r1 * rows, c0 * rows : c1 * rows]

    def factors(q):
        left = (block(0, 1, 0, 1), block(1, 2, 0, 2), block(2, 4, 0, 3), block(3, 4, 3, 4))[q]
        fwd[0 : left.shape[0], 0 : 3 * left.shape[1]] = hhl(left, 1)
        if q == 1:
            back = jnp.concatenate([block(1, 4, 1, 2).T, block(1, 4, 0, 1).T], axis=0)
        else:
            back = (block(0, 1, 0, 1), None, block(2, 4, 2, 3), block(3, 4, 3, 4))[q].T
        bwd[0 : back.shape[0], 0 : 3 * back.shape[1]] = hhl(back, 1)

    def fold(tile):
        return sum(tile[:, k * lanes : (k + 1) * lanes] for k in range(tile.shape[1] // lanes))

    def send_sum_near():
        cells = jnp.sum(acc[...].reshape(rows // 8, 8, lanes), axis=0)
        near[place] = cells - 0.5 * fold(prior[...])
        for j in range(1, group):
            remote(near.at[place], near.at[place], send_near, recv_near, device(quarter, lax.rem(place + j, group)))

    def send_sum_far():
        if group > 1:
            others = near.at[pl.ds(0, group - 1)]
            await_bytes(others, send_near)
            await_bytes(others, recv_near)
        far[quarter] = jnp.sum(near[...], axis=0)
        for j in range(1, QUARTERS):
            remote(far.at[quarter], far.at[quarter], send_far, recv_far, device(lax.rem(quarter + j, QUARTERS), place))

    ahead = min(AHEAD, chunks)

    def start(chunk, carry):
        spread(chunk)
        return carry

    lax.fori_loop(0, ahead, start, 0)
    acc[...] = jnp.zeros_like(acc)
    for q in range(QUARTERS):
        @pl.when(quarter == q)
        def _(q=q):
            factors(q)

    last = chunks + max(FORWARD_LAG)

    def turn(i, carry):
        @pl.when(i + ahead < chunks)
        def _():
            spread(i + ahead)

        for q in range(QUARTERS):
            @pl.when((quarter == q) & (i < chunks))
            def _(q=q):
                onward(q, i)

            @pl.when((quarter == q) & (i >= FORWARD_LAG[q]) & (i < chunks + FORWARD_LAG[q]))
            def _(q=q):
                forward(q, i - FORWARD_LAG[q])

            @pl.when((quarter == q) & (i >= BACKWARD_LAG[q]) & (i < chunks + BACKWARD_LAG[q]))
            def _(q=q):
                backward(q, i - BACKWARD_LAG[q])

        @pl.when(i == last - 1)
        def _():
            send_sum_near()

        @pl.when(i == last + 1)
        def _():
            send_sum_far()

        return carry

    lax.fori_loop(0, chunks + max(BACKWARD_LAG), turn, 0)

    others = far.at[pl.ds(0, QUARTERS - 1)]
    await_bytes(others, send_far)
    await_bytes(others, recv_far)
    density[...] = jnp.sum(far[...], axis=0)

    away = (slice(None), pl.ds(0, (group - 1) * lines))
    if group > 1:
        for k, src in enumerate((q_hbm, cnt_hbm, exp_hbm)):
            await_bytes(src.at[away], send_in.at[k])
    for slot in range(depth):
        await_collected(slot)

    @pl.when(quarter == 0)
    def _():
        await_bytes(own, send_z.at[1])

    @pl.when(quarter <= 1)
    def _():
        await_bytes(own, send_z.at[0])

    @pl.when(quarter >= 2)
    def _():
        for slot in range(depth):
            await_bytes(res.at[slot], send_r.at[slot])

    @pl.when(quarter == 3)
    def _():
        for slot in range(depth):
            await_bytes(res.at[slot], send_r.at[slot])

    @pl.when((quarter == 1) | (quarter == 2))
    def _():
        for slot in range(depth):
            await_bytes(spare.at[slot], send_s.at[slot])

    if group > 1:
        await_bytes(out_hbm.at[away], recv_g)


def exchange(partly, counts, exposure, east, prior, group):
    planes, all_lines, times = partly.shape
    rows = planes * group
    parts = times // LANES
    chunks = all_lines // group * parts
    depth = min(DEPTH, chunks)
    whole = lambda kind: pltpu.VMEM((chunks, rows, LANES), kind)
    ring = lambda: pltpu.VMEM((depth, rows, LANES), jnp.float32)
    stacked = lambda: pltpu.VMEM((2 * rows, 9 * rows), jnp.bfloat16)
    any_space = pl.BlockSpec(memory_space=pl.ANY)
    in_vmem = pl.BlockSpec(memory_space=pltpu.VMEM)
    dma = pltpu.SemaphoreType.DMA
    return pl.pallas_call(
        functools.partial(kernel, group, parts),
        out_shape=(
            jax.ShapeDtypeStruct(partly.shape, jnp.float32),
            jax.ShapeDtypeStruct((8, LANES), jnp.float32),
        ),
        in_specs=[any_space] * 3 + [in_vmem] * 2,
        out_specs=(any_space, in_vmem),
        scratch_shapes=[whole(jnp.float32) for _ in range(3)]
        + [whole(jnp.int32) for _ in range(2)]
        + [whole(jnp.float32) for _ in range(2)]
        + [ring() for _ in range(3)]
        + [stacked() for _ in range(2)]
        + [
            pltpu.VMEM((rows, LANES), jnp.float32),
            pltpu.VMEM((group, 8, LANES), jnp.float32),
            pltpu.VMEM((QUARTERS, 8, LANES), jnp.float32),
        ]
        + [dma((3,))]
        + [dma((chunks,)) for _ in range(3)]
        + [dma((2,))]
        + [dma((chunks,)) for _ in range(4)]
        + [dma((depth,)) for _ in range(4)]
        + [dma] * 5,
        compiler_params=pltpu.CompilerParams(
            collective_id=0, has_side_effects=True, vmem_limit_bytes=VMEM_BYTES
        ),
    )(partly, counts, exposure, east, prior)


def prepare_kernel(w_ref, north, time, q_ref, squares, left, right):
    @pl.when(pl.program_id(0) == 0)
    def _():
        left[...] = hhl(north[...], 1)
        right[...] = hhl(time[...].T, 0)
        squares[...] = jnp.zeros_like(squares)

    block, lines, times = w_ref.shape
    values = w_ref[...].reshape(block * lines, times)
    squares[...] += jnp.sum((values * values).reshape(-1, 8, times), axis=0)
    partly = dot(hlh(values, 1), right[...])
    for a in range(block):
        q_ref[a] = dot(left[...], hlh(partly[a * lines : (a + 1) * lines], 0))


def finish_kernel(scale, g_ref, w_ref, north, time, terms, out_ref, density, left, right):
    @pl.when(pl.program_id(0) == 0)
    def _():
        left[...] = hhl(north[...].T, 1)
        right[...] = hhl(time[...], 0)
        density[0] = jnp.sum(terms[...]) * scale

    block, lines, times = g_ref.shape
    values = g_ref[...].reshape(block * lines, times)
    partly = dot(hlh(values, 1), right[...])
    for a in range(block):
        adjoint = dot(left[...], hlh(partly[a * lines : (a + 1) * lines], 0))
        out_ref[a] = field_scale * adjoint - w_ref[a]


BLOCK = 2


def planes_spec(lines, times):
    return pl.BlockSpec((BLOCK, lines, times), lambda i: (i, 0, 0))


def fixed_spec(*shape):
    return pl.BlockSpec(shape, lambda i: (0, 0))


def stacked_pair(lines, times):
    return [pltpu.VMEM((lines, 3 * lines), jnp.bfloat16), pltpu.VMEM((3 * times, times), jnp.bfloat16)]


def prepare(whitened, north, time):
    planes, lines, times = whitened.shape
    return pl.pallas_call(
        prepare_kernel,
        grid=(planes // BLOCK,),
        out_shape=[jax.ShapeDtypeStruct(whitened.shape, jnp.float32), jax.ShapeDtypeStruct((8, times), jnp.float32)],
        in_specs=[planes_spec(lines, times), fixed_spec(lines, lines), fixed_spec(times, times)],
        out_specs=[planes_spec(lines, times), fixed_spec(8, times)],
        scratch_shapes=stacked_pair(lines, times),
    )(whitened, north, time)


def finish(adjoint, whitened, north, time, terms, scale):
    planes, lines, times = whitened.shape
    return pl.pallas_call(
        functools.partial(finish_kernel, scale),
        grid=(planes // BLOCK,),
        out_shape=[jax.ShapeDtypeStruct(whitened.shape, jnp.float32), jax.ShapeDtypeStruct((1,), jnp.float32)],
        in_specs=[planes_spec(lines, times)] * 2
        + [fixed_spec(lines, lines), fixed_spec(times, times), fixed_spec(*terms.shape)],
        out_specs=[planes_spec(lines, times), pl.BlockSpec(memory_space=pltpu.SMEM)],
        scratch_shapes=stacked_pair(lines, times),
    )(adjoint, whitened, north, time, terms)


def per_device(whitened, counts, exposure, cholesky_east, cholesky_north, cholesky_time):
    slabs = lax.axis_size("slab")
    cell_count = whitened.shape[0] * whitened.shape[1] * whitened.shape[2] * slabs
    partly, squares = prepare(whitened, cholesky_north, cholesky_time)
    adjoint, terms = exchange(partly, counts, exposure, cholesky_east, squares, slabs // QUARTERS)
    gradient, density = finish(adjoint, whitened, cholesky_north, cholesky_time, terms, 1.0 / cell_count)
    return (gradient, density)


def solution(mesh):
    placed = (
        P(("chain", "slab"), None, None),
        P(("chain", "slab"), None, None),
        P(("chain", "slab"), None, None),
        P(),
        P(),
        P(),
    )
    return jax.shard_map(
        per_device,
        mesh=mesh,
        in_specs=placed,
        out_specs=(P(("chain", "slab"), None, None), P("chain")),
        check_vma=False,
    )
```

```python
import functools

import jax
import jax.numpy as jnp
from jax import lax
from jax.experimental import pallas as pl
from jax.experimental.pallas import tpu as pltpu
from jax.sharding import PartitionSpec as P

field_scale = 0.6
QUARTERS = 4
LANES = 128
AHEAD = 4
RING = 16
BANDS = 4
SENT = 4
FORWARD_LAG = (2, 4, 0, 0)
BACKWARD_LAG = (10, 8, 4, 1)
VMEM_BYTES = 67043328


def split(values):
    high = values.astype(jnp.bfloat16)
    low = (values - high.astype(jnp.float32)).astype(jnp.bfloat16)
    return high, low


def hhl(matrix, axis):
    high, low = split(matrix)
    return jnp.concatenate([high, high, low], axis=axis)


def hlh(matrix, axis):
    high, low = split(matrix)
    return jnp.concatenate([high, low, high], axis=axis)


def dot(left, right):
    return jnp.dot(left, right, preferred_element_type=jnp.float32)


def kernel(
    group, parts, w_hbm, cnt_hbm, exp_hbm, east, north, time, out_hbm, density,
    held, q_own, squares, left, onto, back, pending, own, f0, f1, cnt, wgt, b0, b1, res, spare, out, fwd, bwd, acc, near, far,
    send_in, recv_p, recv_o, recv_f, recv_b, send_z, send_r, send_g, keep_g, recv_g,
    send_near, recv_near, send_far, recv_far, load_first, load_rest,
):
    slab = lax.axis_index("slab")
    quarter = slab // group
    place = slab % group
    ring = own.shape[0]
    rows = own.shape[1]
    lanes = own.shape[2]
    planes, north_cells, times = held.shape
    lines = north_cells // group
    chunks = lines * parts
    rings = out.shape[0]
    band = north_cells // BANDS
    per_band = band // group * parts

    first = (slice(None), pl.ds(0, band))
    rest = (slice(None), pl.ds(band, north_cells - band))
    pltpu.make_async_copy(w_hbm.at[first], held.at[first], load_first).start()
    pltpu.make_async_copy(w_hbm.at[rest], held.at[rest], load_rest).start()

    def device(quarter_of, place_of):
        return {"slab": quarter_of * group + place_of}

    barrier = pltpu.get_barrier_semaphore()
    for j in range(1, group):
        pl.semaphore_signal(barrier, inc=1, device_id=device(quarter, lax.rem(place + j, group)), device_id_type=pl.DeviceIdType.MESH)
    for j in range(1, QUARTERS):
        pl.semaphore_signal(barrier, inc=1, device_id=device(lax.rem(quarter + j, QUARTERS), place), device_id_type=pl.DeviceIdType.MESH)
    left[...] = hhl(north[...], 1)
    onto[...] = hhl(time[...].T, 0)
    back[...] = hhl(time[...], 0)
    acc[...] = jnp.zeros_like(acc)
    squares[...] = jnp.zeros_like(squares)
    pl.semaphore_wait(barrier, group + QUARTERS - 2)

    def remote(src, dst, send_sem, recv_sem, target):
        pltpu.make_async_remote_copy(
            src_ref=src, dst_ref=dst, send_sem=send_sem, recv_sem=recv_sem,
            device_id=target, device_id_type=pl.DeviceIdType.MESH,
        ).start()

    def await_bytes(ref, sem):
        pltpu.make_async_copy(ref, ref, sem).wait()

    def await_slots(count, sem):
        if count:
            await_bytes(own.at[pl.ds(0, count)], sem)

    def slot_of(chunk):
        return lax.rem(chunk, ring)

    def line_of(chunk, place_of):
        return chunk // parts * group + place_of

    def times_of(chunk):
        return pl.ds(pl.multiple_of(lax.rem(chunk, parts) * lanes, lanes), lanes)

    def spread(chunk, arrays):
        mine = pl.ds(place * planes, planes)
        slot = slot_of(chunk)
        for k in arrays:
            src, dst, recv = ((q_own, own, recv_p), (cnt_hbm, cnt, recv_o), (exp_hbm, wgt, recv_o))[k]
            for j in range(1, group):
                to = lax.rem(place + j, group)
                remote(
                    src.at[:, line_of(chunk, to), times_of(chunk)], dst.at[slot, mine],
                    send_in.at[k], recv.at[slot], device(quarter, to),
                )
            pltpu.make_async_copy(
                src.at[:, line_of(chunk, place), times_of(chunk)], dst.at[slot, mine], recv.at[slot]
            ).start()

    def square(cells):
        squares[...] += jnp.sum((cells * cells).reshape(-1, 8, times), axis=0)

    def begin():
        few = min(planes, 4)

        def some(i, carry):
            mixed = []
            for k in range(few):
                cells = held[i * few + k, 0:band]
                square(cells)
                mixed.append(dot(hhl(north[0:band, 0:band], 1), hlh(cells, 0)))
            partly = dot(hlh(jnp.concatenate(mixed, axis=0), 1), onto[...])
            for k in range(few):
                q_own[i * few + k, 0:band] = partly[k * band : (k + 1) * band]
            return carry

        lax.fori_loop(0, planes // few, some, 0)

    def proceed(step):
        part = planes // per_band
        rows_of = pl.ds(pl.multiple_of((step // per_band + 1) * band, band), band)
        for k in range(part):
            plane = lax.rem(step, per_band) * part + k
            square(held[plane, rows_of])
            mixed = dot(left[rows_of], hlh(held[plane], 0))
            q_own[plane, rows_of] = dot(hlh(mixed, 1), onto[...])

    def collect(line, slot):
        there = (slice(None), line * group + place)
        for j in range(1, group):
            to = lax.rem(place + j, group)
            remote(out.at[slot, pl.ds(to * planes, planes)], out_hbm.at[there], send_g.at[slot], recv_g, device(quarter, to))
        pltpu.make_async_copy(out.at[slot, pl.ds(place * planes, planes)], out_hbm.at[there], keep_g.at[slot]).start()

    def await_collected(line):
        slot = lax.rem(line, rings)
        if group > 1:
            await_bytes(out.at[slot, pl.ds(0, (group - 1) * planes)], send_g.at[slot])
        await_bytes(out.at[slot, pl.ds(0, planes)], keep_g.at[slot])

    def onward(q, chunk):
        slot = slot_of(chunk)
        await_bytes(own.at[slot], recv_p.at[slot])
        if q == 0:
            remote(own.at[slot], f1.at[slot], send_z.at[slot], recv_f.at[slot], device(2, place))
            remote(own.at[slot], f0.at[slot], send_z.at[slot], recv_f.at[slot], device(1, place))
        if q == 1:
            remote(own.at[slot], f0.at[slot], send_z.at[slot], recv_f.at[slot], device(2, place))

    def await_onward(q, chunk):
        slot = slot_of(chunk)
        await_slots((2, 1, 0, 0)[q], send_z.at[slot])

    def await_residual(q, chunk):
        slot = slot_of(chunk)
        await_slots((0, 0, 2, 2)[q], send_r.at[slot])

    def forward(q, chunk):
        slot = slot_of(chunk)
        await_slots(2, recv_o.at[slot])
        await_slots((0, 1, 2, 1)[q], recv_f.at[slot])

        @pl.when(chunk >= ring)
        def _():
            await_residual(q, chunk)

        terms = ((own,), (f0, own), (f1, f0, own), (own,))[q]
        high_low = hlh(jnp.concatenate([ref[slot] for ref in terms], axis=0), 0)
        count = 2 if q == 2 else 1
        field = dot(fwd[0 : count * rows, 0 : 3 * len(terms) * rows], high_low)
        if q == 2:
            spare[slot] = field[rows:]
            field = field[:rows]
        if q == 3:
            field = field + f0[slot]
        log_rate = field_scale * field
        observed = cnt[slot].astype(jnp.float32)
        intensity = wgt[slot].astype(jnp.float32) * jnp.exp(log_rate)
        acc[...] += observed * log_rate - intensity
        res[slot] = observed - intensity
        if q == 2:
            remote(spare.at[slot], f0.at[slot], send_r.at[slot], recv_f.at[slot], device(3, place))
            remote(res.at[slot], b0.at[slot], send_r.at[slot], recv_b.at[slot], device(1, place))
        if q == 3:
            remote(res.at[slot], b1.at[slot], send_r.at[slot], recv_b.at[slot], device(1, place))
            remote(res.at[slot], b0.at[slot], send_r.at[slot], recv_b.at[slot], device(2, place))

    def await_partial(q, chunk):
        slot = slot_of(chunk)
        if q == 1:
            await_bytes(spare.at[slot], send_r.at[slot])

    def backward(q, chunk):
        slot = slot_of(chunk)
        await_slots((1, 2, 1, 0)[q], recv_b.at[slot])

        @pl.when(chunk >= ring)
        def _():
            await_partial(q, chunk)

        terms = [res[slot]]
        if q in (1, 2):
            terms.append(b0[slot])
        if q == 1:
            terms.append(b1[slot])
        high_low = hlh(jnp.concatenate(terms, axis=0), 0)
        count = 2 if q == 1 else 1
        value = dot(bwd[0 : count * rows, 0 : 3 * len(terms) * rows], high_low)
        if q == 1:
            spare[slot] = value[rows:]
            remote(spare.at[slot], b0.at[slot], send_r.at[slot], recv_b.at[slot], device(0, place))
            value = value[:rows]
        if q == 0:
            value = value + b0[slot]
        pending[:, times_of(chunk)] = value

        @pl.when(lax.rem(chunk, parts) == parts - 1)
        def _():
            line = chunk // parts

            @pl.when(line >= rings)
            def _():
                await_collected(line)

            into = lax.rem(line, rings)
            out[into] = dot(hlh(pending[...], 1), back[...])
            collect(line, into)

    def block(r0, r1, c0, c1):
        return east[r0 * rows : r1 * rows, c0 * rows : c1 * rows]

    def factors(q):
        left = (block(0, 1, 0, 1), block(1, 2, 0, 2), block(2, 4, 0, 3), block(3, 4, 3, 4))[q]
        fwd[0 : left.shape[0], 0 : 3 * left.shape[1]] = hhl(left, 1)
        if q == 1:
            back = jnp.concatenate([block(1, 4, 1, 2).T, block(1, 4, 0, 1).T], axis=0)
        else:
            back = (block(0, 1, 0, 1), None, block(2, 4, 2, 3), block(3, 4, 3, 4))[q].T
        bwd[0 : back.shape[0], 0 : 3 * back.shape[1]] = hhl(back, 1)

    def fold(tile):
        return sum(tile[:, k * lanes : (k + 1) * lanes] for k in range(tile.shape[1] // lanes))

    def send_sum_near():
        cells = jnp.sum(acc[...].reshape(rows // 8, 8, lanes), axis=0)
        near[place] = cells - 0.5 * fold(squares[...])
        for j in range(1, group):
            remote(near.at[place], near.at[place], send_near, recv_near, device(quarter, lax.rem(place + j, group)))

    def send_sum_far():
        if group > 1:
            others = near.at[pl.ds(0, group - 1)]
            await_bytes(others, send_near)
            await_bytes(others, recv_near)
        far[quarter] = jnp.sum(near[...], axis=0)
        for j in range(1, QUARTERS):
            remote(far.at[quarter], far.at[quarter], send_far, recv_far, device(lax.rem(quarter + j, QUARTERS), place))

    ahead = min(AHEAD, chunks)

    def start(arrays):
        def body(chunk, carry):
            spread(chunk, arrays)
            return carry

        lax.fori_loop(0, ahead, body, 0)

    start((1, 2))
    await_bytes(held.at[first], load_first)
    begin()
    start((0,))
    await_bytes(held.at[rest], load_rest)
    last = chunks + max(FORWARD_LAG)

    for q in range(QUARTERS):
        @pl.when(quarter == q)
        def _(q=q):
            factors(q)

            def turn(i, carry):
                @pl.when(i + ahead < chunks)
                def _():
                    spread(i + ahead, (0, 1, 2))

                @pl.when((i >= SENT) & (i < chunks + SENT))
                def _():
                    await_onward(q, i - SENT)

                @pl.when(i < chunks)
                def _():
                    onward(q, i)

                @pl.when((i >= FORWARD_LAG[q]) & (i < chunks + FORWARD_LAG[q]))
                def _():
                    forward(q, i - FORWARD_LAG[q])

                @pl.when((i >= BACKWARD_LAG[q]) & (i < chunks + BACKWARD_LAG[q]))
                def _():
                    backward(q, i - BACKWARD_LAG[q])

                @pl.when(i == last - 1)
                def _():
                    send_sum_near()

                @pl.when(i == last + 1)
                def _():
                    send_sum_far()

                @pl.when(i < ahead)
                def _():
                    proceed(i)

                @pl.when(i + ahead < (BANDS - 1) * per_band)
                def _():
                    proceed(i + ahead)

                return carry

            lax.fori_loop(0, chunks + max(BACKWARD_LAG), turn, 0)

            def drain(chunk, carry):
                await_residual(q, chunk)
                await_partial(q, chunk)
                return carry

            lax.fori_loop(max(chunks - ring, 0), chunks, drain, 0)

    def collected(line, carry):
        await_collected(line)
        return carry

    lax.fori_loop(max(lines - rings, 0), lines, collected, 0)

    others = far.at[pl.ds(0, QUARTERS - 1)]
    await_bytes(others, send_far)
    await_bytes(others, recv_far)
    density[...] = jnp.sum(far[...], axis=0)

    away = (slice(None), pl.ds(0, (group - 1) * lines))
    if group > 1:
        for k, src in enumerate((q_own, cnt_hbm, exp_hbm)):
            await_bytes(src.at[away], send_in.at[k])
        await_bytes(out_hbm.at[away], recv_g)


def exchange(whitened, counts, exposure, east, north, time, group):
    planes, lines, times = whitened.shape
    rows = planes * group
    parts = times // LANES
    ring = lambda kind: pltpu.VMEM((RING, rows, LANES), kind)
    stacked = lambda: pltpu.VMEM((2 * rows, 9 * rows), jnp.bfloat16)
    any_space = pl.BlockSpec(memory_space=pl.ANY)
    in_vmem = pl.BlockSpec(memory_space=pltpu.VMEM)
    dma = pltpu.SemaphoreType.DMA
    return pl.pallas_call(
        functools.partial(kernel, group, parts),
        out_shape=(
            jax.ShapeDtypeStruct(whitened.shape, jnp.float32),
            jax.ShapeDtypeStruct((8, LANES), jnp.float32),
        ),
        in_specs=[any_space] * 3 + [in_vmem] * 3,
        out_specs=(any_space, in_vmem),
        scratch_shapes=[pltpu.VMEM(whitened.shape, jnp.float32) for _ in range(2)]
        + [pltpu.VMEM((8, times), jnp.float32), pltpu.VMEM((lines, 3 * lines), jnp.bfloat16)]
        + [pltpu.VMEM((3 * times, times), jnp.bfloat16) for _ in range(2)]
        + [pltpu.VMEM((rows, times), jnp.float32)]
        + [ring(jnp.float32) for _ in range(3)]
        + [ring(jnp.int32) for _ in range(2)]
        + [ring(jnp.float32) for _ in range(4)]
        + [pltpu.VMEM((RING // parts, rows, times), jnp.float32)]
        + [stacked() for _ in range(2)]
        + [
            pltpu.VMEM((rows, LANES), jnp.float32),
            pltpu.VMEM((group, 8, LANES), jnp.float32),
            pltpu.VMEM((QUARTERS, 8, LANES), jnp.float32),
        ]
        + [dma((3,))]
        + [dma((RING,)) for _ in range(8)]
        + [dma] * 7,
        compiler_params=pltpu.CompilerParams(
            collective_id=0, has_side_effects=True, vmem_limit_bytes=VMEM_BYTES
        ),
    )(whitened, counts, exposure, east, north, time)


def finish_kernel(scale, h_ref, w_ref, north, terms, out_ref, density, left):
    @pl.when(pl.program_id(0) == 0)
    def _():
        left[...] = hhl(north[...].T, 1)
        density[0] = jnp.sum(terms[...]) * scale

    for a in range(h_ref.shape[0]):
        adjoint = dot(left[...], hlh(h_ref[a], 0))
        out_ref[a] = field_scale * adjoint - w_ref[a]


def finish(partly, whitened, north, terms, scale):
    planes, lines, times = whitened.shape
    block = min(planes, 8)
    some = pl.BlockSpec((block, lines, times), lambda i: (i, 0, 0))
    fixed = lambda array: pl.BlockSpec(array.shape, lambda i: (0, 0))
    return pl.pallas_call(
        functools.partial(finish_kernel, scale),
        grid=(planes // block,),
        out_shape=[jax.ShapeDtypeStruct(whitened.shape, jnp.float32), jax.ShapeDtypeStruct((1,), jnp.float32)],
        in_specs=[some] * 2 + [fixed(north), fixed(terms)],
        out_specs=[some, pl.BlockSpec(memory_space=pltpu.SMEM)],
        scratch_shapes=[pltpu.VMEM((lines, 3 * lines), jnp.bfloat16)],
    )(partly, whitened, north, terms)


def per_device(whitened, counts, exposure, cholesky_east, cholesky_north, cholesky_time):
    slabs = lax.axis_size("slab")
    cell_count = whitened.shape[0] * whitened.shape[1] * whitened.shape[2] * slabs
    partly, terms = exchange(
        whitened, counts, exposure, cholesky_east, cholesky_north, cholesky_time, slabs // QUARTERS
    )
    gradient, density = finish(partly, whitened, cholesky_north, terms, 1.0 / cell_count)
    return (gradient, density)


def solution(mesh):
    placed = (
        P(("chain", "slab"), None, None),
        P(("chain", "slab"), None, None),
        P(("chain", "slab"), None, None),
        P(),
        P(),
        P(),
    )
    return jax.shard_map(
        per_device,
        mesh=mesh,
        in_specs=placed,
        out_specs=(P(("chain", "slab"), None, None), P("chain")),
        check_vma=False,
    )
```

```python
import functools

import jax
import jax.numpy as jnp
from jax import lax
from jax.experimental import pallas as pl
from jax.experimental.pallas import tpu as pltpu
from jax.sharding import PartitionSpec as P

field_scale = 0.6
QUARTERS = 4
LANES = 128
AHEAD = 4
EARLY = 3
RING = 16
BANDS = 4
SENT = 4
FORWARD_LAG = (2, 4, 1, 0)
BACKWARD_LAG = (10, 9, 6, 4)
VMEM_BYTES = 67043328


def split(values):
    high = values.astype(jnp.bfloat16)
    low = (values - high.astype(jnp.float32)).astype(jnp.bfloat16)
    return high, low


def hhl(matrix, axis):
    high, low = split(matrix)
    return jnp.concatenate([high, high, low], axis=axis)


def hlh(matrix, axis):
    high, low = split(matrix)
    return jnp.concatenate([high, low, high], axis=axis)


def dot(left, right):
    return jnp.dot(left, right, preferred_element_type=jnp.float32)


def kernel(
    group, parts, w_hbm, cnt_hbm, exp_hbm, east, north, time, out_hbm, density,
    held, q_own, squares, left, onto, back, pending, own, f0, f1, cnt, wgt, b0, b1, res, spare, out, fwd, bwd, acc, near, far,
    send_in, recv_p, recv_o, recv_f, recv_b, send_z, send_r, send_g, keep_g, recv_g,
    send_near, recv_near, send_far, recv_far, load_first, load_rest,
):
    slab = lax.axis_index("slab")
    quarter = slab // group
    place = slab % group
    ring = own.shape[0]
    rows = own.shape[1]
    lanes = own.shape[2]
    planes, north_cells, times = held.shape
    lines = north_cells // group
    chunks = lines * parts
    rings = out.shape[0]
    band = north_cells // BANDS
    per_band = band // group * parts

    first = (slice(None), pl.ds(0, band))
    rest = (slice(None), pl.ds(band, north_cells - band))
    pltpu.make_async_copy(w_hbm.at[first], held.at[first], load_first).start()
    pltpu.make_async_copy(w_hbm.at[rest], held.at[rest], load_rest).start()

    def device(quarter_of, place_of):
        return {"slab": quarter_of * group + place_of}

    barrier = pltpu.get_barrier_semaphore()
    for j in range(1, group):
        pl.semaphore_signal(barrier, inc=1, device_id=device(quarter, lax.rem(place + j, group)), device_id_type=pl.DeviceIdType.MESH)
    for j in range(1, QUARTERS):
        pl.semaphore_signal(barrier, inc=1, device_id=device(lax.rem(quarter + j, QUARTERS), place), device_id_type=pl.DeviceIdType.MESH)
    left[...] = hhl(north[...], 1)
    onto[...] = hhl(time[...].T, 0)
    back[...] = hhl(time[...], 0)
    acc[...] = jnp.zeros_like(acc)
    squares[...] = jnp.zeros_like(squares)
    pl.semaphore_wait(barrier, group + QUARTERS - 2)

    def remote(src, dst, send_sem, recv_sem, target):
        pltpu.make_async_remote_copy(
            src_ref=src, dst_ref=dst, send_sem=send_sem, recv_sem=recv_sem,
            device_id=target, device_id_type=pl.DeviceIdType.MESH,
        ).start()

    def await_bytes(ref, sem):
        pltpu.make_async_copy(ref, ref, sem).wait()

    def await_slots(count, sem):
        if count:
            await_bytes(own.at[pl.ds(0, count)], sem)

    def slot_of(chunk):
        return lax.rem(chunk, ring)

    def line_of(chunk, place_of):
        return chunk // parts * group + place_of

    def times_of(chunk):
        return pl.ds(pl.multiple_of(lax.rem(chunk, parts) * lanes, lanes), lanes)

    def spread(chunk, arrays):
        mine = pl.ds(place * planes, planes)
        slot = slot_of(chunk)
        for k in arrays:
            src, dst, recv = ((q_own, own, recv_p), (cnt_hbm, cnt, recv_o), (exp_hbm, wgt, recv_o))[k]
            for j in range(1, group):
                to = lax.rem(place + j, group)
                remote(
                    src.at[:, line_of(chunk, to), times_of(chunk)], dst.at[slot, mine],
                    send_in.at[k], recv.at[slot], device(quarter, to),
                )
            pltpu.make_async_copy(
                src.at[:, line_of(chunk, place), times_of(chunk)], dst.at[slot, mine], recv.at[slot]
            ).start()

    def square(cells):
        squares[...] += jnp.sum((cells * cells).reshape(-1, 8, times), axis=0)

    def begin():
        few = min(planes, 4)

        def some(i, carry):
            mixed = []
            for k in range(few):
                cells = held[i * few + k, 0:band]
                square(cells)
                mixed.append(dot(hhl(north[0:band, 0:band], 1), hlh(cells, 0)))
            partly = dot(hlh(jnp.concatenate(mixed, axis=0), 1), onto[...])
            for k in range(few):
                q_own[i * few + k, 0:band] = partly[k * band : (k + 1) * band]
            return carry

        lax.fori_loop(0, planes // few, some, 0)

    def proceed(step):
        part = planes // per_band
        rows_of = pl.ds(pl.multiple_of((step // per_band + 1) * band, band), band)
        for k in range(part):
            plane = lax.rem(step, per_band) * part + k
            square(held[plane, rows_of])
            mixed = dot(left[rows_of], hlh(held[plane], 0))
            q_own[plane, rows_of] = dot(hlh(mixed, 1), onto[...])

    def collect(line, slot):
        there = (slice(None), line * group + place)
        for j in range(1, group):
            to = lax.rem(place + j, group)
            remote(out.at[slot, pl.ds(to * planes, planes)], out_hbm.at[there], send_g.at[slot], recv_g, device(quarter, to))
        pltpu.make_async_copy(out.at[slot, pl.ds(place * planes, planes)], out_hbm.at[there], keep_g.at[slot]).start()

    def await_collected(line):
        slot = lax.rem(line, rings)
        if group > 1:
            await_bytes(out.at[slot, pl.ds(0, (group - 1) * planes)], send_g.at[slot])
        await_bytes(out.at[slot, pl.ds(0, planes)], keep_g.at[slot])

    def onward(q, chunk):
        slot = slot_of(chunk)
        await_bytes(own.at[slot], recv_p.at[slot])
        if q == 0:
            remote(own.at[slot], f1.at[slot], send_z.at[slot], recv_f.at[slot], device(2, place))
            remote(own.at[slot], f0.at[slot], send_z.at[slot], recv_f.at[slot], device(1, place))
        if q == 1:
            remote(own.at[slot], f0.at[slot], send_z.at[slot], recv_f.at[slot], device(2, place))

    def await_onward(q, chunk):
        slot = slot_of(chunk)
        await_slots((2, 1, 0, 0)[q], send_z.at[slot])

    def await_residual(q, chunk):
        slot = slot_of(chunk)
        await_slots((0, 0, 2, 2)[q], send_r.at[slot])

    def forward(q, chunk):
        slot = slot_of(chunk)
        await_slots(2, recv_o.at[slot])
        await_slots((0, 1, 2, 1)[q], recv_f.at[slot])

        @pl.when(chunk >= ring)
        def _():
            await_residual(q, chunk)

        terms = ((own,), (f0, own), (f1, f0, own), (own,))[q]
        high_low = hlh(jnp.concatenate([ref[slot] for ref in terms], axis=0), 0)
        count = 2 if q == 2 else 1
        field = dot(fwd[0 : count * rows, 0 : 3 * len(terms) * rows], high_low)
        if q == 2:
            spare[slot] = field[rows:]
            field = field[:rows]
        if q == 3:
            field = field + f0[slot]
        log_rate = field_scale * field
        observed = cnt[slot].astype(jnp.float32)
        intensity = wgt[slot].astype(jnp.float32) * jnp.exp(log_rate)
        acc[...] += observed * log_rate - intensity
        res[slot] = observed - intensity
        if q == 2:
            remote(spare.at[slot], f0.at[slot], send_r.at[slot], recv_f.at[slot], device(3, place))
            remote(res.at[slot], b0.at[slot], send_r.at[slot], recv_b.at[slot], device(1, place))
        if q == 3:
            remote(res.at[slot], b1.at[slot], send_r.at[slot], recv_b.at[slot], device(1, place))
            remote(res.at[slot], b0.at[slot], send_r.at[slot], recv_b.at[slot], device(2, place))

    def await_partial(q, chunk):
        slot = slot_of(chunk)
        if q == 1:
            await_bytes(spare.at[slot], send_r.at[slot])

    def backward(q, chunk):
        slot = slot_of(chunk)
        await_slots((1, 2, 1, 0)[q], recv_b.at[slot])

        @pl.when(chunk >= ring)
        def _():
            await_partial(q, chunk)

        terms = [res[slot]]
        if q in (1, 2):
            terms.append(b0[slot])
        if q == 1:
            terms.append(b1[slot])
        high_low = hlh(jnp.concatenate(terms, axis=0), 0)
        count = 2 if q == 1 else 1
        value = dot(bwd[0 : count * rows, 0 : 3 * len(terms) * rows], high_low)
        if q == 1:
            spare[slot] = value[rows:]
            remote(spare.at[slot], b0.at[slot], send_r.at[slot], recv_b.at[slot], device(0, place))
            value = value[:rows]
        if q == 0:
            value = value + b0[slot]
        pending[:, times_of(chunk)] = value

        @pl.when(lax.rem(chunk, parts) == parts - 1)
        def _():
            line = chunk // parts

            @pl.when(line >= rings)
            def _():
                await_collected(line)

            into = lax.rem(line, rings)
            out[into] = dot(hlh(pending[...], 1), back[...])
            collect(line, into)

    def block(r0, r1, c0, c1):
        return east[r0 * rows : r1 * rows, c0 * rows : c1 * rows]

    def factors(q):
        left = (block(0, 1, 0, 1), block(1, 2, 0, 2), block(2, 4, 0, 3), block(3, 4, 3, 4))[q]
        fwd[0 : left.shape[0], 0 : 3 * left.shape[1]] = hhl(left, 1)
        if q == 1:
            back = jnp.concatenate([block(1, 4, 1, 2).T, block(1, 4, 0, 1).T], axis=0)
        else:
            back = (block(0, 1, 0, 1), None, block(2, 4, 2, 3), block(3, 4, 3, 4))[q].T
        bwd[0 : back.shape[0], 0 : 3 * back.shape[1]] = hhl(back, 1)

    def fold(tile):
        return sum(tile[:, k * lanes : (k + 1) * lanes] for k in range(tile.shape[1] // lanes))

    def send_sum_near():
        cells = jnp.sum(acc[...].reshape(rows // 8, 8, lanes), axis=0)
        near[place] = cells - 0.5 * fold(squares[...])
        for j in range(1, group):
            remote(near.at[place], near.at[place], send_near, recv_near, device(quarter, lax.rem(place + j, group)))

    def send_sum_far():
        if group > 1:
            others = near.at[pl.ds(0, group - 1)]
            await_bytes(others, send_near)
            await_bytes(others, recv_near)
        far[quarter] = jnp.sum(near[...], axis=0)
        for j in range(1, QUARTERS):
            remote(far.at[quarter], far.at[quarter], send_far, recv_far, device(lax.rem(quarter + j, QUARTERS), place))

    ahead = min(AHEAD, chunks)

    def start(lower, upper, arrays):
        def body(chunk, carry):
            spread(chunk, arrays)
            return carry

        lax.fori_loop(lower, upper, body, 0)

    early = min(EARLY, ahead)
    start(0, early, (1, 2))
    await_bytes(held.at[first], load_first)
    begin()
    start(0, early, (0,))
    start(early, ahead, (0, 1, 2))
    await_bytes(held.at[rest], load_rest)
    last = chunks + max(FORWARD_LAG)

    for q in range(QUARTERS):
        @pl.when(quarter == q)
        def _(q=q):
            factors(q)

            def turn(i, carry):
                @pl.when(i + ahead < chunks)
                def _():
                    spread(i + ahead, (0, 1, 2))

                @pl.when((i >= SENT) & (i < chunks + SENT))
                def _():
                    await_onward(q, i - SENT)

                @pl.when(i < chunks)
                def _():
                    onward(q, i)

                @pl.when((i >= FORWARD_LAG[q]) & (i < chunks + FORWARD_LAG[q]))
                def _():
                    forward(q, i - FORWARD_LAG[q])

                @pl.when((i >= BACKWARD_LAG[q]) & (i < chunks + BACKWARD_LAG[q]))
                def _():
                    backward(q, i - BACKWARD_LAG[q])

                @pl.when(i == last - 1)
                def _():
                    send_sum_near()

                @pl.when(i == last + 1)
                def _():
                    send_sum_far()

                @pl.when(i < ahead)
                def _():
                    proceed(i)

                @pl.when(i + ahead < (BANDS - 1) * per_band)
                def _():
                    proceed(i + ahead)

                return carry

            lax.fori_loop(0, chunks + max(BACKWARD_LAG), turn, 0)

            def drain(chunk, carry):
                await_residual(q, chunk)
                await_partial(q, chunk)
                return carry

            lax.fori_loop(max(chunks - ring, 0), chunks, drain, 0)

    def collected(line, carry):
        await_collected(line)
        return carry

    lax.fori_loop(max(lines - rings, 0), lines, collected, 0)

    others = far.at[pl.ds(0, QUARTERS - 1)]
    await_bytes(others, send_far)
    await_bytes(others, recv_far)
    density[...] = jnp.sum(far[...], axis=0)

    away = (slice(None), pl.ds(0, (group - 1) * lines))
    if group > 1:
        for k, src in enumerate((q_own, cnt_hbm, exp_hbm)):
            await_bytes(src.at[away], send_in.at[k])
        await_bytes(out_hbm.at[away], recv_g)


def exchange(whitened, counts, exposure, east, north, time, group):
    planes, lines, times = whitened.shape
    rows = planes * group
    parts = times // LANES
    ring = lambda kind: pltpu.VMEM((RING, rows, LANES), kind)
    stacked = lambda: pltpu.VMEM((2 * rows, 9 * rows), jnp.bfloat16)
    any_space = pl.BlockSpec(memory_space=pl.ANY)
    in_vmem = pl.BlockSpec(memory_space=pltpu.VMEM)
    dma = pltpu.SemaphoreType.DMA
    return pl.pallas_call(
        functools.partial(kernel, group, parts),
        out_shape=(
            jax.ShapeDtypeStruct(whitened.shape, jnp.float32),
            jax.ShapeDtypeStruct((8, LANES), jnp.float32),
        ),
        in_specs=[any_space] * 3 + [in_vmem] * 3,
        out_specs=(any_space, in_vmem),
        scratch_shapes=[pltpu.VMEM(whitened.shape, jnp.float32) for _ in range(2)]
        + [pltpu.VMEM((8, times), jnp.float32), pltpu.VMEM((lines, 3 * lines), jnp.bfloat16)]
        + [pltpu.VMEM((3 * times, times), jnp.bfloat16) for _ in range(2)]
        + [pltpu.VMEM((rows, times), jnp.float32)]
        + [ring(jnp.float32) for _ in range(3)]
        + [ring(jnp.int32) for _ in range(2)]
        + [ring(jnp.float32) for _ in range(4)]
        + [pltpu.VMEM((RING // parts, rows, times), jnp.float32)]
        + [stacked() for _ in range(2)]
        + [
            pltpu.VMEM((rows, LANES), jnp.float32),
            pltpu.VMEM((group, 8, LANES), jnp.float32),
            pltpu.VMEM((QUARTERS, 8, LANES), jnp.float32),
        ]
        + [dma((3,))]
        + [dma((RING,)) for _ in range(8)]
        + [dma] * 7,
        compiler_params=pltpu.CompilerParams(
            collective_id=0, has_side_effects=True, vmem_limit_bytes=VMEM_BYTES
        ),
    )(whitened, counts, exposure, east, north, time)


def finish_kernel(scale, h_ref, w_ref, north, terms, out_ref, density, left):
    @pl.when(pl.program_id(0) == 0)
    def _():
        left[...] = hhl(north[...].T, 1)
        density[0] = jnp.sum(terms[...]) * scale

    for a in range(h_ref.shape[0]):
        adjoint = dot(left[...], hlh(h_ref[a], 0))
        out_ref[a] = field_scale * adjoint - w_ref[a]


def finish(partly, whitened, north, terms, scale):
    planes, lines, times = whitened.shape
    block = min(planes, 16)
    some = pl.BlockSpec((block, lines, times), lambda i: (i, 0, 0))
    fixed = lambda array: pl.BlockSpec(array.shape, lambda i: (0, 0))
    return pl.pallas_call(
        functools.partial(finish_kernel, scale),
        grid=(planes // block,),
        out_shape=[jax.ShapeDtypeStruct(whitened.shape, jnp.float32), jax.ShapeDtypeStruct((1,), jnp.float32)],
        in_specs=[some] * 2 + [fixed(north), fixed(terms)],
        out_specs=[some, pl.BlockSpec(memory_space=pltpu.SMEM)],
        scratch_shapes=[pltpu.VMEM((lines, 3 * lines), jnp.bfloat16)],
    )(partly, whitened, north, terms)


def per_device(whitened, counts, exposure, cholesky_east, cholesky_north, cholesky_time):
    slabs = lax.axis_size("slab")
    cell_count = whitened.shape[0] * whitened.shape[1] * whitened.shape[2] * slabs
    partly, terms = exchange(
        whitened, counts, exposure, cholesky_east, cholesky_north, cholesky_time, slabs // QUARTERS
    )
    gradient, density = finish(partly, whitened, cholesky_north, terms, 1.0 / cell_count)
    return (gradient, density)


def solution(mesh):
    placed = (
        P(("chain", "slab"), None, None),
        P(("chain", "slab"), None, None),
        P(("chain", "slab"), None, None),
        P(),
        P(),
        P(),
    )
    return jax.shard_map(
        per_device,
        mesh=mesh,
        in_specs=placed,
        out_specs=(P(("chain", "slab"), None, None), P("chain")),
        check_vma=False,
    )
```

```python
import functools

import jax
import jax.numpy as jnp
from jax import lax
from jax.experimental import pallas as pl
from jax.experimental.pallas import tpu as pltpu
from jax.sharding import PartitionSpec as P

field_scale = 0.6
QUARTERS = 4
LANES = 128
AHEAD = 3
EARLY = 3
RING = 12
BANDS = 4
SENT = 4
FORWARD_LAG = (2, 4, 1, 0)
BACKWARD_LAG = (9, 8, 6, 4)
VMEM_BYTES = 67043328


def split(values):
    high = values.astype(jnp.bfloat16)
    low = (values - high.astype(jnp.float32)).astype(jnp.bfloat16)
    return high, low


def hhl(matrix, axis):
    high, low = split(matrix)
    return jnp.concatenate([high, high, low], axis=axis)


def hlh(matrix, axis):
    high, low = split(matrix)
    return jnp.concatenate([high, low, high], axis=axis)


def dot(left, right):
    return jnp.dot(left, right, preferred_element_type=jnp.float32)


def kernel(
    group, parts, w_hbm, cnt_hbm, exp_hbm, east_hbm, north, time, out_hbm, density,
    held, q_own, squares, left, onto, back, pending, own, f0, f1, cnt, wgt, b0, b1, res, spare, out, fwd, bwd, acc, near, far,
    send_in, recv_p, recv_o, recv_f, recv_b, send_z, send_r, send_g, keep_g, recv_g,
    send_near, recv_near, send_far, recv_far, load_first, load_rest, load_east, east,
):
    slab = lax.axis_index("slab")
    quarter = slab // group
    place = slab % group
    ring = own.shape[0]
    rows = own.shape[1]
    lanes = own.shape[2]
    planes, north_cells, times = held.shape
    lines = north_cells // group
    chunks = lines * parts
    rings = out.shape[0]
    band = north_cells // BANDS
    per_band = band // group * parts

    first = (slice(None), pl.ds(0, band))
    rest = (slice(None), pl.ds(band, north_cells - band))
    pltpu.make_async_copy(w_hbm.at[first], held.at[first], load_first).start()
    pltpu.make_async_copy(w_hbm.at[rest], held.at[rest], load_rest).start()
    pltpu.make_async_copy(east_hbm, east, load_east).start()

    def device(quarter_of, place_of):
        return {"slab": quarter_of * group + place_of}

    barrier = pltpu.get_barrier_semaphore()
    for j in range(1, group):
        pl.semaphore_signal(barrier, inc=1, device_id=device(quarter, lax.rem(place + j, group)), device_id_type=pl.DeviceIdType.MESH)
    for j in range(1, QUARTERS):
        pl.semaphore_signal(barrier, inc=1, device_id=device(lax.rem(quarter + j, QUARTERS), place), device_id_type=pl.DeviceIdType.MESH)
    left[...] = hhl(north[...], 1)
    onto[...] = hhl(time[...].T, 0)
    back[...] = hhl(time[...], 0)
    acc[...] = jnp.zeros_like(acc)
    squares[...] = jnp.zeros_like(squares)
    pl.semaphore_wait(barrier, group + QUARTERS - 2)

    def remote(src, dst, send_sem, recv_sem, target):
        pltpu.make_async_remote_copy(
            src_ref=src, dst_ref=dst, send_sem=send_sem, recv_sem=recv_sem,
            device_id=target, device_id_type=pl.DeviceIdType.MESH,
        ).start()

    def await_bytes(ref, sem):
        pltpu.make_async_copy(ref, ref, sem).wait()

    def await_slots(count, sem):
        if count:
            await_bytes(own.at[pl.ds(0, count)], sem)

    def slot_of(chunk):
        return lax.rem(chunk, ring)

    def line_of(chunk, place_of):
        return chunk // parts * group + place_of

    def times_of(chunk):
        return pl.ds(pl.multiple_of(lax.rem(chunk, parts) * lanes, lanes), lanes)

    def spread(chunk, arrays):
        mine = pl.ds(place * planes, planes)
        slot = slot_of(chunk)
        for k in arrays:
            src, dst, recv = ((q_own, own, recv_p), (cnt_hbm, cnt, recv_o), (exp_hbm, wgt, recv_o))[k]
            for j in range(1, group):
                to = lax.rem(place + j, group)
                remote(
                    src.at[:, line_of(chunk, to), times_of(chunk)], dst.at[slot, mine],
                    send_in.at[k], recv.at[slot], device(quarter, to),
                )
            pltpu.make_async_copy(
                src.at[:, line_of(chunk, place), times_of(chunk)], dst.at[slot, mine], recv.at[slot]
            ).start()

    def square(cells):
        squares[...] += jnp.sum((cells * cells).reshape(-1, 8, times), axis=0)

    def begin():
        few = min(planes, 4)

        def some(i, carry):
            mixed = []
            for k in range(few):
                cells = held[i * few + k, 0:band]
                square(cells)
                mixed.append(dot(hhl(north[0:band, 0:band], 1), hlh(cells, 0)))
            partly = dot(hlh(jnp.concatenate(mixed, axis=0), 1), onto[...])
            for k in range(few):
                q_own[i * few + k, 0:band] = partly[k * band : (k + 1) * band]
            return carry

        lax.fori_loop(0, planes // few, some, 0)

    def proceed(step):
        part = planes // per_band
        rows_of = pl.ds(pl.multiple_of((step // per_band + 1) * band, band), band)
        for k in range(part):
            plane = lax.rem(step, per_band) * part + k
            square(held[plane, rows_of])
            mixed = dot(left[rows_of], hlh(held[plane], 0))
            q_own[plane, rows_of] = dot(hlh(mixed, 1), onto[...])

    def collect(line, slot):
        there = (slice(None), line * group + place)
        for j in range(1, group):
            to = lax.rem(place + j, group)
            remote(out.at[slot, pl.ds(to * planes, planes)], out_hbm.at[there], send_g.at[slot], recv_g, device(quarter, to))
        pltpu.make_async_copy(out.at[slot, pl.ds(place * planes, planes)], out_hbm.at[there], keep_g.at[slot]).start()

    def await_collected(line):
        slot = lax.rem(line, rings)
        if group > 1:
            await_bytes(out.at[slot, pl.ds(0, (group - 1) * planes)], send_g.at[slot])
        await_bytes(out.at[slot, pl.ds(0, planes)], keep_g.at[slot])

    def onward(q, chunk):
        slot = slot_of(chunk)
        await_bytes(own.at[slot], recv_p.at[slot])
        if q == 0:
            remote(own.at[slot], f1.at[slot], send_z.at[slot], recv_f.at[slot], device(2, place))
            remote(own.at[slot], f0.at[slot], send_z.at[slot], recv_f.at[slot], device(1, place))
        if q == 1:
            remote(own.at[slot], f0.at[slot], send_z.at[slot], recv_f.at[slot], device(2, place))

    def await_onward(q, chunk):
        slot = slot_of(chunk)
        await_slots((2, 1, 0, 0)[q], send_z.at[slot])

    def await_residual(q, chunk):
        slot = slot_of(chunk)
        await_slots((0, 0, 2, 2)[q], send_r.at[slot])

    def forward(q, chunk):
        slot = slot_of(chunk)
        await_slots(2, recv_o.at[slot])
        await_slots((0, 1, 2, 1)[q], recv_f.at[slot])

        @pl.when(chunk >= ring)
        def _():
            await_residual(q, chunk)

        terms = ((own,), (f0, own), (f1, f0, own), (own,))[q]
        high_low = hlh(jnp.concatenate([ref[slot] for ref in terms], axis=0), 0)
        count = 2 if q == 2 else 1
        field = dot(fwd[0 : count * rows, 0 : 3 * len(terms) * rows], high_low)
        if q == 2:
            spare[slot] = field[rows:]
            field = field[:rows]
        if q == 3:
            field = field + f0[slot]
        log_rate = field_scale * field
        observed = cnt[slot].astype(jnp.float32)
        intensity = wgt[slot].astype(jnp.float32) * jnp.exp(log_rate)
        acc[...] += observed * log_rate - intensity
        res[slot] = observed - intensity
        if q == 2:
            remote(spare.at[slot], f0.at[slot], send_r.at[slot], recv_f.at[slot], device(3, place))
            remote(res.at[slot], b0.at[slot], send_r.at[slot], recv_b.at[slot], device(1, place))
        if q == 3:
            remote(res.at[slot], b1.at[slot], send_r.at[slot], recv_b.at[slot], device(1, place))
            remote(res.at[slot], b0.at[slot], send_r.at[slot], recv_b.at[slot], device(2, place))

    def await_partial(q, chunk):
        slot = slot_of(chunk)
        if q == 1:
            await_bytes(spare.at[slot], send_r.at[slot])

    def backward(q, chunk):
        slot = slot_of(chunk)
        await_slots((1, 2, 1, 0)[q], recv_b.at[slot])

        @pl.when(chunk >= ring)
        def _():
            await_partial(q, chunk)

        terms = [res[slot]]
        if q in (1, 2):
            terms.append(b0[slot])
        if q == 1:
            terms.append(b1[slot])
        high_low = hlh(jnp.concatenate(terms, axis=0), 0)
        count = 2 if q == 1 else 1
        value = dot(bwd[0 : count * rows, 0 : 3 * len(terms) * rows], high_low)
        if q == 1:
            spare[slot] = value[rows:]
            remote(spare.at[slot], b0.at[slot], send_r.at[slot], recv_b.at[slot], device(0, place))
            value = value[:rows]
        if q == 0:
            value = value + b0[slot]
        pending[:, times_of(chunk)] = value

        @pl.when(lax.rem(chunk, parts) == parts - 1)
        def _():
            line = chunk // parts

            @pl.when(line >= rings)
            def _():
                await_collected(line)

            into = lax.rem(line, rings)
            out[into] = dot(hlh(pending[...], 1), back[...])
            collect(line, into)

    def block(r0, r1, c0, c1):
        return east[r0 * rows : r1 * rows, c0 * rows : c1 * rows]

    def factors(q):
        left = (block(0, 1, 0, 1), block(1, 2, 0, 2), block(2, 4, 0, 3), block(3, 4, 3, 4))[q]
        fwd[0 : left.shape[0], 0 : 3 * left.shape[1]] = hhl(left, 1)
        if q == 1:
            back = jnp.concatenate([block(1, 4, 1, 2).T, block(1, 4, 0, 1).T], axis=0)
        else:
            back = (block(0, 1, 0, 1), None, block(2, 4, 2, 3), block(3, 4, 3, 4))[q].T
        bwd[0 : back.shape[0], 0 : 3 * back.shape[1]] = hhl(back, 1)

    def fold(tile):
        return sum(tile[:, k * lanes : (k + 1) * lanes] for k in range(tile.shape[1] // lanes))

    def send_sum_near():
        cells = jnp.sum(acc[...].reshape(rows // 8, 8, lanes), axis=0)
        near[place] = cells - 0.5 * fold(squares[...])
        for j in range(1, group):
            remote(near.at[place], near.at[place], send_near, recv_near, device(quarter, lax.rem(place + j, group)))

    def send_sum_far():
        if group > 1:
            others = near.at[pl.ds(0, group - 1)]
            await_bytes(others, send_near)
            await_bytes(others, recv_near)
        far[quarter] = jnp.sum(near[...], axis=0)
        for j in range(1, QUARTERS):
            remote(far.at[quarter], far.at[quarter], send_far, recv_far, device(lax.rem(quarter + j, QUARTERS), place))

    ahead = min(AHEAD, chunks)

    def start(lower, upper, arrays):
        def body(chunk, carry):
            spread(chunk, arrays)
            return carry

        lax.fori_loop(lower, upper, body, 0)

    early = min(EARLY, ahead)
    start(0, early, (1, 2))
    await_bytes(held.at[first], load_first)
    begin()
    start(0, early, (0,))
    start(early, ahead, (0, 1, 2))
    await_bytes(held.at[rest], load_rest)
    await_bytes(east, load_east)
    last = chunks + max(FORWARD_LAG)

    for q in range(QUARTERS):
        @pl.when(quarter == q)
        def _(q=q):
            factors(q)

            def turn(i, carry):
                @pl.when(i + ahead < chunks)
                def _():
                    spread(i + ahead, (0, 1, 2))

                @pl.when((i >= SENT) & (i < chunks + SENT))
                def _():
                    await_onward(q, i - SENT)

                @pl.when(i < chunks)
                def _():
                    onward(q, i)

                @pl.when((i >= FORWARD_LAG[q]) & (i < chunks + FORWARD_LAG[q]))
                def _():
                    forward(q, i - FORWARD_LAG[q])

                @pl.when((i >= BACKWARD_LAG[q]) & (i < chunks + BACKWARD_LAG[q]))
                def _():
                    backward(q, i - BACKWARD_LAG[q])

                @pl.when(i == last - 1)
                def _():
                    send_sum_near()

                @pl.when(i == last + 1)
                def _():
                    send_sum_far()

                @pl.when(i < ahead)
                def _():
                    proceed(i)

                @pl.when(i + ahead < (BANDS - 1) * per_band)
                def _():
                    proceed(i + ahead)

                return carry

            lax.fori_loop(0, chunks + max(BACKWARD_LAG), turn, 0)

            def drain(chunk, carry):
                await_residual(q, chunk)
                await_partial(q, chunk)
                return carry

            lax.fori_loop(max(chunks - ring, 0), chunks, drain, 0)

    def collected(line, carry):
        await_collected(line)
        return carry

    lax.fori_loop(max(lines - rings, 0), lines, collected, 0)

    others = far.at[pl.ds(0, QUARTERS - 1)]
    await_bytes(others, send_far)
    await_bytes(others, recv_far)
    density[...] = jnp.sum(far[...], axis=0)

    away = (slice(None), pl.ds(0, (group - 1) * lines))
    if group > 1:
        for k, src in enumerate((q_own, cnt_hbm, exp_hbm)):
            await_bytes(src.at[away], send_in.at[k])
        await_bytes(out_hbm.at[away], recv_g)


def exchange(whitened, counts, exposure, east, north, time, group):
    planes, lines, times = whitened.shape
    rows = planes * group
    parts = times // LANES
    ring = lambda kind: pltpu.VMEM((RING, rows, LANES), kind)
    stacked = lambda: pltpu.VMEM((2 * rows, 9 * rows), jnp.bfloat16)
    any_space = pl.BlockSpec(memory_space=pl.ANY)
    in_vmem = pl.BlockSpec(memory_space=pltpu.VMEM)
    dma = pltpu.SemaphoreType.DMA
    return pl.pallas_call(
        functools.partial(kernel, group, parts),
        out_shape=(
            jax.ShapeDtypeStruct(whitened.shape, jnp.float32),
            jax.ShapeDtypeStruct((8, LANES), jnp.float32),
        ),
        in_specs=[any_space] * 4 + [in_vmem] * 2,
        out_specs=(any_space, in_vmem),
        scratch_shapes=[pltpu.VMEM(whitened.shape, jnp.float32) for _ in range(2)]
        + [pltpu.VMEM((8, times), jnp.float32), pltpu.VMEM((lines, 3 * lines), jnp.bfloat16)]
        + [pltpu.VMEM((3 * times, times), jnp.bfloat16) for _ in range(2)]
        + [pltpu.VMEM((rows, times), jnp.float32)]
        + [ring(jnp.float32) for _ in range(3)]
        + [ring(jnp.int32) for _ in range(2)]
        + [ring(jnp.float32) for _ in range(4)]
        + [pltpu.VMEM((RING // parts, rows, times), jnp.float32)]
        + [stacked() for _ in range(2)]
        + [
            pltpu.VMEM((rows, LANES), jnp.float32),
            pltpu.VMEM((group, 8, LANES), jnp.float32),
            pltpu.VMEM((QUARTERS, 8, LANES), jnp.float32),
        ]
        + [dma((3,))]
        + [dma((RING,)) for _ in range(8)]
        + [dma] * 8
        + [pltpu.VMEM(east.shape, jnp.float32)],
        compiler_params=pltpu.CompilerParams(
            collective_id=0, has_side_effects=True, vmem_limit_bytes=VMEM_BYTES
        ),
    )(whitened, counts, exposure, east, north, time)


def finish_kernel(scale, h_ref, w_ref, north, terms, out_ref, density, left):
    @pl.when(pl.program_id(0) == 0)
    def _():
        left[...] = hhl(north[...].T, 1)
        density[0] = jnp.sum(terms[...]) * scale

    for a in range(h_ref.shape[0]):
        adjoint = dot(left[...], hlh(h_ref[a], 0))
        out_ref[a] = field_scale * adjoint - w_ref[a]


def finish(partly, whitened, north, terms, scale):
    planes, lines, times = whitened.shape
    block = min(planes, 16)
    some = pl.BlockSpec((block, lines, times), lambda i: (i, 0, 0))
    fixed = lambda array: pl.BlockSpec(array.shape, lambda i: (0, 0))
    return pl.pallas_call(
        functools.partial(finish_kernel, scale),
        grid=(planes // block,),
        out_shape=[jax.ShapeDtypeStruct(whitened.shape, jnp.float32), jax.ShapeDtypeStruct((1,), jnp.float32)],
        in_specs=[some] * 2 + [fixed(north), fixed(terms)],
        out_specs=[some, pl.BlockSpec(memory_space=pltpu.SMEM)],
        scratch_shapes=[pltpu.VMEM((lines, 3 * lines), jnp.bfloat16)],
    )(partly, whitened, north, terms)


def per_device(whitened, counts, exposure, cholesky_east, cholesky_north, cholesky_time):
    slabs = lax.axis_size("slab")
    cell_count = whitened.shape[0] * whitened.shape[1] * whitened.shape[2] * slabs
    partly, terms = exchange(
        whitened, counts, exposure, cholesky_east, cholesky_north, cholesky_time, slabs // QUARTERS
    )
    gradient, density = finish(partly, whitened, cholesky_north, terms, 1.0 / cell_count)
    return (gradient, density)


def solution(mesh):
    placed = (
        P(("chain", "slab"), None, None),
        P(("chain", "slab"), None, None),
        P(("chain", "slab"), None, None),
        P(),
        P(),
        P(),
    )
    return jax.shard_map(
        per_device,
        mesh=mesh,
        in_specs=placed,
        out_specs=(P(("chain", "slab"), None, None), P("chain")),
        check_vma=False,
    )
```
